32 devices in a mesh: shard: 8 (over z, x), replica: 4 (over y, core).
Axes of the slice: x: 2, y: 2, z: 4, core: 2. Of those that a mesh axis runs over, the one named last changes fastest.
Arguments:
- samples: bfloat16 [2048, 480, 128], P(('shard', 'replica')), may hold values from -6 to 6
- counts: int32 [2048], P(('shard', 'replica')), may hold values from 1 to 480
- buckets: int32 [2048, 480], P(('shard', 'replica')), may hold values from 0 to 127
- block_series: int32 [2048], P(('shard', 'replica')), may hold values from 0 to 63, as said below
- owner_map: int32 [64], replicated, may hold values from 0 to 63
Outputs:
- cold_stats: float32 [8, 4, 128, 4, 8, 128], P('shard', 'replica')
- sketches: float32 [64, 128, 128], P(('shard', 'replica'))
- live_rows: float32 [64], P(('shard', 'replica'))
The draws below stay inside these ranges and needn't reach their ends.
Inputs may be any that keep to these rules, and one draw needn't show every extreme that they name: `block_series`: owner_map is a permutation of 0 to 63. With owner = owner_map[series] // 8, the 64 blocks of one device name at most 16 blocks of any one owner, and in every draw some owner gets exactly 16 blocks from every device.
All inputs are finite; a program needn't handle non-finite values.
Results may differ from the reference program's by a relative error of at most 0.0003.
Values may be sent and summed in bfloat16 or wider, within the bound.
No kernel may reach another device: no remote copies, remote signals or barrier semaphores. Data moves between devices by JAX's collectives and lax.ppermute only.
A program may use at most 192 MiB of HBM per device.

```python
import jax
import jax.numpy as jnp
from jax import lax

LANES = 128
BINS = 128
MINUTES = 8
BLK_DEV = 64
SAMPLES = 480
BLOCKS = 2048
SER_OWN = 8
SERIES = 64
CAP = 16
HEAVY = 1
N_SHARD = 8
N_REPLICA = 4


def routing(key):
    owner_map = jax.random.permutation(jax.random.fold_in(key, 11), SERIES).astype(jnp.int32)
    inverse = jnp.argsort(owner_map).astype(jnp.int32)
    order = jax.random.permutation(jax.random.fold_in(key, 12), N_SHARD)
    heavy = jnp.zeros((N_SHARD,), jnp.int32).at[order[:HEAVY]].set(1)
    devices = N_SHARD * N_REPLICA
    width = N_SHARD * CAP
    candidate = jnp.arange(width, dtype=jnp.int32) // CAP
    noise = jax.random.randint(jax.random.fold_in(key, 13), (devices, width), 0, 1 << 20)
    score = (noise + heavy[candidate][None, :] * (1 << 21)) * width + jnp.arange(width, dtype=jnp.int32)[None, :]
    _, picked = lax.top_k(score, BLK_DEV)
    owners = candidate[picked]
    shuffle = jax.random.randint(jax.random.fold_in(key, 14), (devices, BLK_DEV), 0, 1 << 20) * BLK_DEV
    shuffle = shuffle + jnp.arange(BLK_DEV, dtype=jnp.int32)[None, :]
    owners = jnp.take_along_axis(owners, jnp.argsort(shuffle, axis=1), axis=1)
    local = jax.random.randint(jax.random.fold_in(key, 15), (devices, BLK_DEV), 0, SER_OWN)
    series = inverse[(owners * SER_OWN + local).reshape(-1)]
    return (owner_map, series.astype(jnp.int32))


def draw_owner_map(key, part):
    return routing(key)[0]


def draw_block_series(key, part):
    return routing(key)[1]


def with_ends(result, stream_key, smallest, high):
    shape = result.shape
    index_at = [jax.random.randint(jax.random.fold_in(stream_key, axis), (), 0, shape[axis]) for axis in range(len(shape))]
    result = result.at[tuple(index_at)].set(smallest)
    longest = shape.index(max(shape))
    index_at[longest] = (index_at[longest] + 1) % shape[longest]
    return result.at[tuple(index_at)].set(high)


def block_levels(stream_key, extent, cuts, low, largest):
    factor_of = 1.0
    for dim, shards_of in cuts:
        heights = jax.random.uniform(jax.random.fold_in(jax.random.fold_in(stream_key, 6), dim), (shards_of,), jnp.float32, low / len(cuts), largest / len(cuts))
        factor_of = factor_of * jnp.repeat(jnp.exp(heights), extent[dim] // shards_of).reshape((-1,) + (1,) * (len(extent) - 1 - dim))
    return factor_of


def bell_draw(stream_key, dims, scale, bound, pieces=(), kind=jnp.bfloat16):
    array = jax.random.normal(stream_key, dims, jnp.float32) * scale
    if len(pieces) > 0:
        array = block_levels(stream_key, dims, pieces, -0.22, 0.18) * array
    return jnp.clip(array, min=-bound, max=bound).astype(kind)


def setup_inputs(seed: int = 0) -> dict:
    key_list = jax.random.split(jax.random.key(seed), 6)
    return {
        "samples": bell_draw(key_list[0], (BLOCKS, SAMPLES, LANES), 1.0, 6.0, ((0, 32),)),
        "counts": with_ends(jax.random.randint(key_list[1], (BLOCKS,), 1, SAMPLES + 1), jax.random.fold_in(key_list[1], 1), 1, SAMPLES).astype(jnp.int32),
        "buckets": with_ends(jax.random.randint(key_list[2], (BLOCKS, SAMPLES), 0, BINS), jax.random.fold_in(key_list[2], 1), 0, BINS - 1).astype(jnp.int32),
        "block_series": draw_block_series(jax.random.fold_in(key_list[5], 71), 0),
        "owner_map": draw_owner_map(jax.random.fold_in(key_list[5], 71), 0),
    }


def minute_stats(values, counts):
    blocks, samples, lanes = values.shape
    minutes = samples // 60
    steps = jnp.arange(samples, dtype=jnp.int32)
    live = (steps[None, :] < counts[:, None]).reshape(blocks, minutes, 60, 1)
    data = values.astype(jnp.float32).reshape(blocks, minutes, 60, lanes)
    count = jnp.sum(jnp.where(live, jnp.float32(1.0), jnp.float32(0.0)), axis=2)
    count = jnp.broadcast_to(count, (blocks, minutes, lanes))
    total = jnp.sum(jnp.where(live, data, jnp.float32(0.0)), axis=2)
    lowest = jnp.min(jnp.where(live, data, jnp.inf), axis=2)
    highest = jnp.max(jnp.where(live, data, -jnp.inf), axis=2)
    filled = count > 0
    lowest = jnp.where(filled, lowest, jnp.float32(0.0))
    highest = jnp.where(filled, highest, jnp.float32(0.0))
    return jnp.stack([lowest, highest, total, count], axis=1)


def reference(samples, counts, buckets, block_series, owner_map):
    groups = N_SHARD * N_REPLICA
    position = owner_map[block_series].astype(jnp.int32)
    owner = position // SER_OWN
    grouped = owner.reshape(N_SHARD, N_REPLICA, BLK_DEV)
    index = jnp.arange(BLK_DEV, dtype=jnp.int32)
    same = (grouped[..., :, None] == grouped[..., None, :]) & (index[None, :] < index[:, None])
    rank = jnp.sum(same.astype(jnp.int32), axis=-1)
    source = jnp.broadcast_to(jnp.arange(N_SHARD, dtype=jnp.int32)[:, None, None], rank.shape)
    replica = jnp.broadcast_to(jnp.arange(N_REPLICA, dtype=jnp.int32)[None, :, None], rank.shape)
    values_g = samples.reshape(groups, BLK_DEV, SAMPLES, LANES)
    counts_g = counts.reshape(groups, BLK_DEV)
    stats = lax.map(lambda item: minute_stats(item[0], item[1]), (values_g, counts_g))
    stats = stats.reshape(N_SHARD, N_REPLICA, BLK_DEV, 4, MINUTES, LANES)
    cold = jnp.zeros((N_SHARD, N_REPLICA, N_SHARD * CAP, 4, MINUTES, LANES), jnp.float32)
    cold = cold.at[grouped, replica, source * CAP + rank].set(stats)
    steps = jnp.arange(SAMPLES, dtype=jnp.int32)
    marks_g = buckets.reshape(groups, BLK_DEV, SAMPLES)
    places_g = position.reshape(groups, BLK_DEV)

    def accumulate(carry, item):
        values, marks, live_count, places = item
        live = steps[None, :] < live_count[:, None]
        ids = jnp.where(live, places[:, None] * BINS + marks, SERIES * BINS).astype(jnp.int32)
        data = values.astype(jnp.float32).reshape(-1, LANES)
        return carry + jax.ops.segment_sum(data, ids.reshape(-1), num_segments=SERIES * BINS + 1), None

    start = jnp.zeros((SERIES * BINS + 1, LANES), jnp.float32)
    total, _ = lax.scan(accumulate, start, (values_g, marks_g, counts_g, places_g))
    sketches = total[:SERIES * BINS].reshape(SERIES, BINS, LANES)
    live_rows = jax.ops.segment_sum(counts.astype(jnp.float32), position, num_segments=SERIES)
    return cold, sketches, live_rows
```

```python
import functools

import jax
import jax.numpy as jnp
from jax import lax
from jax.experimental import pallas as pl
from jax.experimental.pallas import tpu as pltpu
from jax.sharding import PartitionSpec as P

BINS = 128
MINUTE = 60
SUB = 8
PACK = 16
LIMIT = 6.0
STEPS16 = 32767.0
LIVE_BASE = 16384
VMEM_LIMIT = 56 * 2**20

ANY = pl.BlockSpec(memory_space=pl.ANY)
SMEM = pl.BlockSpec(memory_space=pltpu.SMEM)
VMEM = pl.BlockSpec(memory_space=pltpu.VMEM)


def round_up(n, m):
    return -(-n // m) * m


def to_int16(x):
    return jnp.floor(x + 0.5).astype(jnp.int32).astype(jnp.int16)


class Plan:
    def __init__(self, shards, replicas, series, blocks):
        self.shards, self.replicas, self.series = shards, replicas, series
        self.ser_own = series // shards
        self.ser_dev = self.ser_own // replicas
        self.cap = max(2, (2 * blocks + shards - 1) // shards)
        self.rest = (replicas // 2) * shards
        self.bits = self.rest.bit_length() - 1
        self.half = self.rest * self.ser_dev
        sbits = shards.bit_length() - 1
        assert replicas >= 2 and 2**self.bits == self.rest
        self.order = list(range(sbits, self.bits)) + list(range(sbits))
        self.sum_at = self.cap * 2 * SUB
        self.count_at = self.sum_at + round_up(self.cap * SUB, PACK)
        self.pay_rows = self.count_at + round_up(self.cap, PACK)

    def partner(self, step):
        bit = -1 if step < 0 else self.order[step]
        sbits = self.shards.bit_length() - 1
        if step < 0:
            axis, size, flip = "replica", self.replicas, 1
        elif bit >= sbits:
            axis, size, flip = "replica", self.replicas, 2 << (bit - sbits)
        else:
            axis, size, flip = "shard", self.shards, 1 << bit
        return axis, [(i, i ^ flip) for i in range(size)]

    def count(self, step):
        return (1 << (self.bits - step - 1)) * self.ser_dev

    def rows(self, step):
        n = self.count(step)
        return n * BINS + round_up(n, PACK) + PACK

    def squeeze(self, j, steps):
        out, at = 0, 0
        for bit in range(self.bits):
            if bit not in self.order[:steps]:
                out = out + (((j >> bit) & 1) << at)
                at += 1
        return out

    def spread(self, index, steps):
        out, at = 0, 0
        for bit in range(self.bits):
            if bit not in self.order[:steps]:
                out |= ((index >> at) & 1) << bit
                at += 1
        return out


def reduce_rows(parts, op, row):
    out = list(parts)
    for width in (4, 2, 1):
        low = (row & width) == 0
        merged = []
        for i in range(width):
            a, b = out[i], out[i + width]
            first = jnp.where(low, a, b)
            other = jnp.where(low, b, a)
            up = pltpu.roll(other, SUB - width, 0)
            if width == 4:
                turned = up
            else:
                turned = jnp.where(low, up, pltpu.roll(other, width, 0))
            merged.append(op(first, turned))
        out = merged
    return out[0]


def minute_ends(x, count, minutes, op, worst, row16):
    lanes = x.shape[1]
    fill = jnp.full((PACK, lanes), worst, x.dtype)
    tiles = []
    for v in range(x.shape[0] // PACK):
        live = row16 < (count - PACK * v)
        tiles.append(jnp.where(live, x[PACK * v : PACK * (v + 1)], fill))
    out = []
    for m in range(minutes):
        lo, hi = m * MINUTE, (m + 1) * MINUTE
        total = None
        for v in range(lo // PACK, -(-hi // PACK)):
            tile = tiles[v]
            if v * PACK < lo:
                tile = jnp.where(row16 >= lo - v * PACK, tile, fill)
            if (v + 1) * PACK > hi:
                tile = jnp.where(row16 < hi - v * PACK, tile, fill)
            total = tile if total is None else op(total, tile)
        wide = total.astype(jnp.float32)
        out.append(op(wide[:SUB], wide[SUB:]))
    return out


def ingest_kernel(
    plan, counts, series, omap, buckets, samples, send, keep, pay_out,
    buf, acc, pay, sums, tallies, used, sem, out_sem,
):
    blocks, rows, lanes = buf.shape
    minutes = rows // MINUTE
    me = lax.axis_index("replica")
    copies = lambda b: pltpu.make_async_copy(samples.at[b], buf.at[b], sem.at[b])

    @pl.loop(0, blocks)
    def _(b):
        copies(b).start()

    for o in range(plan.shards):
        used[o] = 0
    tallies[...] = jnp.zeros_like(tallies)

    @pl.loop(0, 2 * plan.half)
    def _(i):
        acc[i] = jnp.zeros((BINS, lanes), jnp.float32)

    when = lax.broadcasted_iota(jnp.int32, (1, rows), 1)
    which = when // MINUTE
    levels = lax.broadcasted_iota(jnp.int32, (BINS + PACK, rows), 0)
    row = lax.broadcasted_iota(jnp.int32, (SUB, lanes), 0)
    row16 = lax.broadcasted_iota(jnp.int32, (PACK, lanes), 0)
    place = row * lanes + lax.broadcasted_iota(jnp.int32, (SUB, lanes), 1)

    def step(b, live_total):
        count = counts[b]
        p = omap[series[b]]
        o = p // plan.ser_own
        local = p - o * plan.ser_own
        r = local // plan.ser_dev
        d = local - r * plan.ser_dev
        c = used[o]
        used[o] = c + 1
        away = (r ^ me) & 1
        j = ((r >> 1) * plan.shards + o) * plan.ser_dev + d
        copies(b).wait()
        x = buf[b]
        live = when < count
        marks = jnp.where(live, buckets[pl.ds(b, 1), :], -1)
        whole = jnp.where(live, which, -1)
        marks = jnp.broadcast_to(marks, (BINS, rows))
        whole = jnp.broadcast_to(whole, (PACK, rows))
        hot = jnp.concatenate(
            [
                (marks == levels[:BINS]).astype(jnp.float32).astype(jnp.bfloat16),
                (whole == levels[:PACK]).astype(jnp.float32).astype(jnp.bfloat16),
            ],
            axis=0,
        )
        out = jnp.dot(hot, x, preferred_element_type=jnp.float32)
        at = away * plan.half + j
        acc[at] += out[:BINS]
        low = minute_ends(x, count, minutes, jnp.minimum, jnp.inf, row16)
        high = minute_ends(x, count, minutes, jnp.maximum, -jnp.inf, row16)
        low = reduce_rows(low, jnp.minimum, row)
        high = reduce_rows(high, jnp.maximum, row)
        n = jnp.clip(count - MINUTE * row, 0, MINUTE).astype(jnp.float32)
        filled = n > 0
        scale = STEPS16 / LIMIT
        ends = jnp.concatenate(
            [jnp.where(filled, low, 0.0), jnp.where(filled, high, 0.0)], axis=0
        )
        pay[o, pl.ds(pl.multiple_of(c * 2 * SUB, 2 * SUB), 2 * SUB), :] = to_int16(ends * scale)
        mean = out[BINS : BINS + SUB] / jnp.maximum(n, 1.0)
        mean = jnp.clip(mean, -LIMIT, LIMIT) * scale
        at8 = pl.multiple_of((o * plan.cap + c) * SUB, SUB)
        sums[pl.ds(at8, SUB), :] = jnp.floor(mean + 0.5).astype(jnp.int32)
        tallies[pl.ds(o * round_up(plan.cap, PACK) + c, 1), :] = jnp.full((1, lanes), count, jnp.int32)
        return live_total + jnp.where(place == p, count, 0)

    live_total = lax.fori_loop(0, blocks, step, jnp.zeros((SUB, lanes), jnp.int32))
    for side in range(2):
        acc[2 * plan.half + side, pl.ds(0, SUB), :] = live_total.astype(jnp.float32)
    outs = []
    for side, target in ((1, send), (0, keep)):
        outs.append(pltpu.make_async_copy(
            acc.at[pl.ds(side * plan.half, plan.half)],
            target.at[pl.ds(0, plan.half)], out_sem.at[2 * side]))
        outs.append(pltpu.make_async_copy(
            acc.at[2 * plan.half + side, pl.ds(0, SUB), :],
            target.at[plan.half, pl.ds(0, SUB), :], out_sem.at[2 * side + 1]))
    for copy in outs:
        copy.start()
    sum_rows = plan.cap * SUB
    tally_rows = round_up(plan.cap, PACK)
    for o in range(plan.shards):
        pay[o, plan.sum_at : plan.sum_at + sum_rows, :] = sums[
            o * sum_rows : (o + 1) * sum_rows, :
        ].astype(jnp.int16)
        pay[o, plan.count_at : plan.pay_rows, :] = tallies[
            o * tally_rows : (o + 1) * tally_rows, :
        ].astype(jnp.int16)
    copy = pltpu.make_async_copy(pay, pay_out, out_sem.at[4])
    copy.start()
    outs.append(copy)
    for copy in outs:
        copy.wait()


def ingest(plan, samples, counts, buckets, series, omap):
    blocks, rows, lanes = samples.shape
    half = jax.ShapeDtypeStruct((plan.half + 1, BINS, lanes), jnp.float32)
    pay = jax.ShapeDtypeStruct((plan.shards, plan.pay_rows, lanes), jnp.int16)
    return pl.pallas_call(
        functools.partial(ingest_kernel, plan),
        out_shape=(half, half, pay),
        in_specs=[SMEM, SMEM, SMEM, VMEM, ANY],
        out_specs=(ANY, ANY, ANY),
        scratch_shapes=[
            pltpu.VMEM((blocks, rows, lanes), jnp.bfloat16),
            pltpu.VMEM((2 * plan.half + 2, BINS, lanes), jnp.float32),
            pltpu.VMEM((plan.shards, plan.pay_rows, lanes), jnp.int16),
            pltpu.VMEM((plan.shards * plan.cap * SUB, lanes), jnp.int32),
            pltpu.VMEM((plan.shards * round_up(plan.cap, PACK), lanes), jnp.int32),
            pltpu.SMEM((plan.shards,), jnp.int32),
            pltpu.SemaphoreType.DMA((blocks,)),
            pltpu.SemaphoreType.DMA((5,)),
        ],
        compiler_params=pltpu.CompilerParams(vmem_limit_bytes=VMEM_LIMIT),
        name="ingest",
    )(counts, series, omap, buckets, samples)


def decode_live(tile):
    low = tile[:SUB].astype(jnp.float32)
    return low + tile[SUB:].astype(jnp.float32) * float(LIVE_BASE)


def exchange_kernel(plan, step, *refs):
    arrays = step + 2
    last = step == plan.bits
    ins, refs = refs[:arrays], refs[arrays:]
    outs, refs = refs[: 2 if last else 1], refs[2 if last else 1 :]
    f32buf, i16buf, f32tail, i16tail, stage, powers, sem, tail_sem, out_sem = refs
    lanes = f32buf.shape[-1]
    mine = (lax.axis_index("replica") >> 1) * plan.shards + lax.axis_index("shard")
    ways = plan.count(step) if not last else plan.ser_dev
    ser_dev = plan.ser_dev
    copies = []
    for g in range(ways // ser_dev):
        base = 0
        for i, bit in enumerate(plan.order[: step + 1]):
            base = base | ((mine ^ (1 << bit if i == step else 0)) & (1 << bit))
        j = base + plan.spread(g, step + 1) if not last else mine
        group = []
        for a in range(arrays):
            if a < 2:
                src = ins[a].at[pl.ds(j * ser_dev, ser_dev)]
                dst = f32buf.at[a, pl.ds(g * ser_dev, ser_dev)]
            else:
                start = pl.multiple_of(plan.squeeze(j, a - 1) * ser_dev * BINS, BINS)
                src = ins[a].at[pl.ds(start, ser_dev * BINS)]
                dst = i16buf.at[a - 2, pl.ds(g * ser_dev * BINS, ser_dev * BINS)]
            group.append((a, pltpu.make_async_copy(src, dst, sem.at[g * arrays + a]), j))
        copies.append(group)
    tails = []
    for a in range(arrays):
        if a < 2:
            src, dst = ins[a].at[plan.half, pl.ds(0, SUB), :], f32tail.at[a]
        else:
            n = plan.count(a - 2)
            size = round_up(n, PACK) + PACK
            src = ins[a].at[pl.ds(n * BINS, size)]
            dst = i16tail.at[a - 2, pl.ds(0, size)]
        tails.append(pltpu.make_async_copy(src, dst, tail_sem.at[a]))
    for copy in tails:
        copy.start()
    for group in copies:
        for _, copy, _ in group:
            copy.start()
    for copy in tails:
        copy.wait()
    live = f32tail[0] + f32tail[1]
    for a in range(2, arrays):
        n = round_up(plan.count(a - 2), PACK)
        live = live + decode_live(i16tail[a - 2, n : n + PACK, :])
        wide = i16tail[a - 2, :n, :].astype(jnp.float32)
        powers[a - 1, :n, :] = jnp.exp2(wide * (1.0 / 64)) * (1.0 / STEPS16)
    written = []
    for g, group in enumerate(copies):
        for _, copy, _ in group:
            copy.wait()
        for d in range(ser_dev):
            at = g * ser_dev + d
            value = f32buf[0, at] + f32buf[1, at]
            for a in range(2, arrays):
                source = plan.squeeze(group[a][2], a - 1) * ser_dev + d
                power = powers[a - 1, pl.ds(source, 1), :]
                coded = i16buf[a - 2, at * BINS : (at + 1) * BINS, :]
                value = value + coded.astype(jnp.float32) * power
            if last:
                outs[0][d] = value
            else:
                top = jnp.max(jnp.abs(value), axis=0, keepdims=True)
                top = jnp.maximum(top, 2.0**-126)
                power = jnp.floor(jnp.log2(top) * 64.0) + 2.0
                powers[0, pl.ds(at, 1), :] = power
                value = value * jnp.exp2(power * (-1.0 / 64)) * STEPS16
                stage[at * BINS : (at + 1) * BINS, :] = to_int16(
                    jnp.clip(value, -STEPS16, STEPS16)
                )
        if not last:
            region = pl.ds(g * ser_dev * BINS, ser_dev * BINS)
            copy = pltpu.make_async_copy(stage.at[region], outs[0].at[region], out_sem.at[g])
            copy.start()
            written.append(copy)
    if last:
        row = lax.broadcasted_iota(jnp.int32, (SUB, lanes), 0)
        place = row * lanes + lax.broadcasted_iota(jnp.int32, (SUB, lanes), 1)
        p = lax.axis_index("shard") * plan.ser_own + lax.axis_index("replica") * ser_dev
        for d in range(ser_dev):
            outs[1][d] = jnp.sum(jnp.where(place == p + d, live, 0.0))
        return
    n = round_up(ways, PACK)
    stage[ways * BINS : ways * BINS + n, :] = powers[0, :n, :].astype(jnp.int32).astype(jnp.int16)
    whole = live.astype(jnp.int32)
    high = whole // LIVE_BASE
    pair = jnp.concatenate([whole - high * LIVE_BASE, high], axis=0)
    stage[ways * BINS + n : ways * BINS + n + PACK, :] = pair.astype(jnp.int16)
    region = pl.ds(ways * BINS, n + PACK)
    copy = pltpu.make_async_copy(stage.at[region], outs[0].at[region], out_sem.at[len(copies)])
    copy.start()
    written.append(copy)
    for copy in written:
        copy.wait()


def exchange(plan, step, arrays, lanes):
    last = step == plan.bits
    ways = plan.ser_dev if last else plan.count(step)
    groups = ways // plan.ser_dev
    coded = max(1, step)
    tail = round_up(plan.count(0), PACK) + PACK
    if last:
        out_shape = (
            jax.ShapeDtypeStruct((plan.ser_dev, BINS, lanes), jnp.float32),
            jax.ShapeDtypeStruct((plan.ser_dev,), jnp.float32),
        )
        out_specs = (VMEM, SMEM)
        stage = PACK
    else:
        stage = plan.rows(step)
        out_shape = jax.ShapeDtypeStruct((stage, lanes), jnp.int16)
        out_specs = ANY
    return pl.pallas_call(
        functools.partial(exchange_kernel, plan, step),
        out_shape=out_shape,
        in_specs=[ANY] * (step + 2),
        out_specs=out_specs,
        scratch_shapes=[
            pltpu.VMEM((2, ways, BINS, lanes), jnp.float32),
            pltpu.VMEM((coded, ways * BINS, lanes), jnp.int16),
            pltpu.VMEM((2, SUB, lanes), jnp.float32),
            pltpu.VMEM((coded, tail, lanes), jnp.int16),
            pltpu.VMEM((stage, lanes), jnp.int16),
            pltpu.VMEM((coded + 1, round_up(plan.count(0), PACK), lanes), jnp.float32),
            pltpu.SemaphoreType.DMA((groups * (step + 2),)),
            pltpu.SemaphoreType.DMA((step + 2,)),
            pltpu.SemaphoreType.DMA((groups + 1,)),
        ],
        compiler_params=pltpu.CompilerParams(vmem_limit_bytes=VMEM_LIMIT),
        name=f"exchange{step}",
    )(*arrays)


def cold_kernel(plan, pay, out):
    lanes = out.shape[-1]
    row = lax.broadcasted_iota(jnp.int32, (SUB, lanes), 0)
    tally = pay[0, plan.count_at : plan.pay_rows, :].astype(jnp.int32)
    for c in range(plan.cap):
        count = jnp.broadcast_to(tally[c : c + 1, :], (SUB, lanes))
        n = jnp.clip(count - MINUTE * row, 0, MINUTE).astype(jnp.float32)
        filled = n > 0
        ends = pay[0, c * 2 * SUB : (c + 1) * 2 * SUB, :].astype(jnp.float32) * (LIMIT / STEPS16)
        mean = pay[0, plan.sum_at + c * SUB : plan.sum_at + (c + 1) * SUB, :].astype(jnp.float32)
        out[c, 0] = jnp.where(filled, ends[:SUB], 0.0)
        out[c, 1] = jnp.where(filled, ends[SUB:], 0.0)
        out[c, 2] = mean * (LIMIT / STEPS16) * n
        out[c, 3] = n


def cold(plan, pay, minutes):
    shards, rows, lanes = pay.shape
    return pl.pallas_call(
        functools.partial(cold_kernel, plan),
        out_shape=jax.ShapeDtypeStruct((shards * plan.cap, 4, minutes, lanes), jnp.float32),
        grid=(shards,),
        in_specs=[pl.BlockSpec((1, rows, lanes), lambda i: (i, 0, 0))],
        out_specs=pl.BlockSpec((plan.cap, 4, minutes, lanes), lambda i: (i, 0, 0, 0)),
        compiler_params=pltpu.CompilerParams(dimension_semantics=("arbitrary",)),
        name="cold",
    )(pay)


def body(samples, counts, buckets, series, omap):
    blocks, rows, lanes = samples.shape
    plan = Plan(lax.axis_size("shard"), lax.axis_size("replica"), omap.shape[0], blocks)
    send, keep, pay = ingest(plan, samples, counts, buckets, series, omap)
    arrays = [keep, lax.ppermute(send, *plan.partner(-1))]
    pay = lax.all_to_all(pay, "shard", split_axis=0, concat_axis=0, tiled=True)
    for step in range(plan.bits):
        coded = exchange(plan, step, arrays, lanes)
        arrays.append(lax.ppermute(coded, *plan.partner(step)))
    sketches, live_rows = exchange(plan, plan.bits, arrays, lanes)
    stats = cold(plan, pay, rows // MINUTE)
    return stats.reshape((1, 1) + stats.shape), sketches, live_rows


def solution(mesh):
    both = ("shard", "replica")
    return jax.shard_map(
        body,
        mesh=mesh,
        in_specs=(P(both, None, None), P(both), P(both, None), P(both), P()),
        out_specs=(
            P("shard", "replica", None, None, None, None),
            P(both, None, None),
            P(both),
        ),
        check_vma=False,
    )
```

```python
import functools

import jax
import jax.numpy as jnp
from jax import lax
from jax.experimental import pallas as pl
from jax.experimental.pallas import tpu as pltpu
from jax.sharding import PartitionSpec as P


BINS = 128
MINUTE = 60
SUB = 8
PACK = 16
LIMIT = 6.0
STEPS16 = 32767.0
LIVE_BASE = 16384
MIB = 2**20

ANY = pl.BlockSpec(memory_space=pl.ANY)
HBM = pl.BlockSpec(memory_space=pltpu.HBM)
SMEM = pl.BlockSpec(memory_space=pltpu.SMEM)
VMEM = pl.BlockSpec(memory_space=pltpu.VMEM)


def round_up(n, m):
    return -(-n // m) * m


def to_int16(x):
    return jnp.floor(x + 0.5).astype(jnp.int32).astype(jnp.int16)


def split(x, n):
    if n & (n - 1) == 0:
        return x >> (n.bit_length() - 1), x & (n - 1)
    return x // n, x - (x // n) * n


class Plan:
    def __init__(self, shards, replicas, series, blocks):
        self.shards, self.replicas, self.series = shards, replicas, series
        self.ser_own = series // shards
        self.ser_dev = self.ser_own // replicas
        self.cap = max(2, (2 * blocks + shards - 1) // shards)
        self.sbits = shards.bit_length() - 1
        self.groups = (replicas // 2) * shards
        self.bits = self.groups.bit_length() - 1
        assert 2**self.bits == self.groups and self.bits > self.sbits > 0 and self.ser_dev == 2
        order = list(range(self.sbits, self.bits)) + list(range(self.sbits))
        first, second = order[0], order[-self.sbits]
        rest = [bit for bit in order if bit not in (first, second)]
        self.orders = ([first, second] + rest, [second, first] + rest)
        self.sum_at = self.cap * 2 * SUB
        self.count_at = self.sum_at + round_up(self.cap * SUB, PACK)
        self.pay_rows = self.count_at + round_up(self.cap, PACK)

    def partner(self, bit):
        if bit < 0:
            axis, size, flip = "replica", self.replicas, 1
        elif bit >= self.sbits:
            axis, size, flip = "replica", self.replicas, 2 << (bit - self.sbits)
        else:
            axis, size, flip = "shard", self.shards, 1 << bit
        return axis, [(i, i ^ flip) for i in range(size)]

    def ways(self, step):
        return 1 << (self.bits - step - 1)

    def count(self, step):
        return self.ways(step) * (1 if step < 2 else 2)

    def rows(self, step):
        n = self.count(step)
        return n * BINS + round_up(n, PACK) + PACK

    def squeeze(self, j, color, steps):
        out, at = 0, 0
        for bit in range(self.bits):
            if bit not in self.orders[color][:steps]:
                out = out + (((j >> bit) & 1) << at)
                at += 1
        return out

    def spread(self, index, color, steps):
        out, at = 0, 0
        for bit in range(self.bits):
            if bit not in self.orders[color][:steps]:
                out = out | (((index >> at) & 1) << bit)
                at += 1
        return out

    def settled(self, mine, color, steps, flip):
        out = 0
        for i, bit in enumerate(self.orders[color][:steps]):
            out = out | ((mine ^ (1 << bit if flip and i == steps - 1 else 0)) & (1 << bit))
        return out

    def position(self, j, away, me, d):
        r = ((j >> self.sbits) << 1) | ((me & 1) ^ away)
        return (j & (self.shards - 1)) * self.ser_own + r * self.ser_dev + d


def reduce_rows(parts, op, row):
    out = list(parts)
    for width in (4, 2, 1):
        low = (row & width) == 0
        merged = []
        for i in range(width):
            a, b = out[i], out[i + width]
            first = jnp.where(low, a, b)
            other = jnp.where(low, b, a)
            up = pltpu.roll(other, SUB - width, 0)
            if width == 4:
                turned = up
            else:
                turned = jnp.where(low, up, pltpu.roll(other, width, 0))
            merged.append(op(first, turned))
        out = merged
    return out[0]


def sketch_kernel(
    plan, chunk, counts, series, omap, buckets, samples,
    send_far, keep_far, send_near, keep_near, marks, buf, total, sem, mark_sem,
):
    blocks, rows, lanes = buf.shape
    me = lax.axis_index("replica")
    mine = (me >> 1) * plan.shards + lax.axis_index("shard")
    fetch = pltpu.make_async_copy(buckets, marks, mark_sem)
    fetch.start()

    def copies(i):
        at = pl.ds(i * chunk, chunk)
        return pltpu.make_async_copy(samples.at[at], buf.at[at], sem.at[i])

    for i in range(blocks // chunk):
        copies(i).start()

    @pl.loop(0, plan.series)
    def _(i):
        total[i] = jnp.zeros((BINS, lanes), jnp.float32)

    sub = lax.broadcasted_iota(jnp.int32, (SUB, lanes), 0)
    place = sub * lanes + lax.broadcasted_iota(jnp.int32, (SUB, lanes), 1)
    when = lax.broadcasted_iota(jnp.int32, (1, rows), 1)
    levels = lax.broadcasted_iota(jnp.int32, (BINS, rows), 0)
    fetch.wait()

    def step(i, live):
        copies(i).wait()
        sums = []
        for u in range(chunk):
            b = i * chunk + u
            p = omap[series[b]]
            mark = jnp.where(when < counts[b], marks[pl.ds(b, 1), :], -1)
            hot = (jnp.broadcast_to(mark, (BINS, rows)) == levels).astype(jnp.float32)
            hot = hot.astype(jnp.bfloat16)
            sums.append((p, jnp.dot(hot, buf[b], preferred_element_type=jnp.float32)))
            live = live + jnp.where(place == p, counts[b], 0)
        for p, out in sums:
            total[p] += out
        return live

    live = lax.fori_loop(0, blocks // chunk, step, jnp.zeros((SUB, lanes), jnp.int32))
    top = plan.groups * BINS
    for ref in (send_far, keep_far):
        ref[top : top + SUB, :] = live.astype(jnp.float32)
    ways = plan.ways(0)
    for far, away, ref in (
        (1, 1, send_far), (1, 0, keep_far), (0, 1, send_near), (0, 0, keep_near),
    ):
        for color in range(2):
            fixed = plan.settled(mine, color, 1, far)

            @pl.loop(0, ways, unroll=4)
            def _(i):
                j = fixed | plan.spread(i, color, 1)
                at = pl.ds(pl.multiple_of((color * ways + i) * BINS, BINS), BINS)
                ref[at, :] = total[plan.position(j, away, me, color)]


def sketch(plan, samples, counts, buckets, series, omap):
    blocks, rows, lanes = samples.shape
    chunk = 8
    far = jax.ShapeDtypeStruct((plan.groups * BINS + SUB, lanes), jnp.float32)
    near = jax.ShapeDtypeStruct((plan.groups * BINS, lanes), jnp.float32)
    return pl.pallas_call(
        functools.partial(sketch_kernel, plan, chunk),
        out_shape=(far, far, near, near),
        in_specs=[SMEM, SMEM, SMEM, HBM, HBM],
        out_specs=(VMEM,) * 4,
        scratch_shapes=[
            pltpu.VMEM((blocks, rows), jnp.int32),
            pltpu.VMEM((blocks, rows, lanes), jnp.bfloat16),
            pltpu.VMEM((plan.series, BINS, lanes), jnp.float32),
            pltpu.SemaphoreType.DMA((blocks // chunk,)),
            pltpu.SemaphoreType.DMA,
        ],
        compiler_params=pltpu.CompilerParams(vmem_limit_bytes=57 * MIB),
        name="sketch",
    )(counts, series, omap, buckets, samples)


def minute_ends(x, minutes, op, worst, row16):
    fill = jnp.full((PACK, x.shape[1]), worst, x.dtype)
    out = []
    for m in range(minutes):
        lo, hi = m * MINUTE, (m + 1) * MINUTE
        total = None
        for v in range(lo // PACK, -(-hi // PACK)):
            tile = x[v * PACK : (v + 1) * PACK]
            if v * PACK < lo:
                tile = jnp.where(row16 >= lo - v * PACK, tile, fill)
            if (v + 1) * PACK > hi:
                tile = jnp.where(row16 < hi - v * PACK, tile, fill)
            total = tile if total is None else op(total, tile)
        wide = total.astype(jnp.float32)
        out.append(op(wide[:SUB], wide[SUB:]))
    return out


def part_ends(x, live, op, worst):
    x = jnp.where(live, x, jnp.full(x.shape, worst, x.dtype))
    total = x[:PACK]
    for v in range(1, x.shape[0] // PACK):
        total = op(total, x[v * PACK : (v + 1) * PACK])
    wide = total.astype(jnp.float32)
    out = op(wide[:SUB], wide[SUB:])
    for width in (4, 2, 1):
        out = op(out, pltpu.roll(out, width, 0))
    return out


def stats_kernel(
    plan, counts, series, omap, samples, after, pay, buf, sums, tallies, used, sem
):
    blocks, rows, lanes = buf.shape
    minutes = rows // MINUTE
    copies = lambda b: pltpu.make_async_copy(samples.at[b], buf.at[b], sem.at[b])

    @pl.loop(0, blocks)
    def _(b):
        copies(b).start()

    for o in range(plan.shards):
        used[o] = 0
    tallies[...] = jnp.zeros_like(tallies)
    when = lax.broadcasted_iota(jnp.int32, (1, rows), 1)
    which = when // MINUTE
    levels = lax.broadcasted_iota(jnp.int32, (PACK, rows), 0)
    sub = lax.broadcasted_iota(jnp.int32, (SUB, lanes), 0)
    row16 = lax.broadcasted_iota(jnp.int32, (PACK, lanes), 0)
    window = round_up(MINUTE + PACK - 4, PACK)
    near = lax.broadcasted_iota(jnp.int32, (window, lanes), 0)
    scale = STEPS16 / LIMIT

    def step(b, _):
        count = counts[b]
        o, _ = split(omap[series[b]], plan.ser_own)
        c = used[o]
        used[o] = c + 1
        copies(b).wait()
        x = buf[b]
        whole = jnp.broadcast_to(jnp.where(when < count, which, -1), (PACK, rows))
        ones = (whole == levels).astype(jnp.float32).astype(jnp.bfloat16)
        total = jnp.dot(ones, x, preferred_element_type=jnp.float32)[:SUB]
        part = count // MINUTE
        start = jnp.minimum((part * MINUTE) // PACK, (rows - window) // PACK) * PACK
        start = pl.multiple_of(start, PACK)
        some = buf[b, pl.ds(start, window), :]
        live = (near >= part * MINUTE - start) & (near < count - start)
        ends = []
        for op, worst in ((jnp.minimum, jnp.inf), (jnp.maximum, -jnp.inf)):
            end = reduce_rows(minute_ends(x, minutes, op, worst, row16), op, sub)
            ends.append(jnp.where(sub == part, part_ends(some, live, op, worst), end))
        n = jnp.clip(count - MINUTE * sub, 0, MINUTE).astype(jnp.float32)
        filled = n > 0
        ends = [jnp.where(filled, end, 0.0) * scale for end in ends]
        at = pl.ds(pl.multiple_of(c * 2 * SUB, 2 * SUB), 2 * SUB)
        pay[o, at, :] = to_int16(jnp.concatenate(ends, axis=0))
        mean = jnp.clip(total / jnp.maximum(n, 1.0), -LIMIT, LIMIT) * scale
        at = pl.ds(pl.multiple_of((o * plan.cap + c) * SUB, SUB), SUB)
        sums[at, :] = jnp.floor(mean + 0.5).astype(jnp.int32)
        at = pl.ds(o * round_up(plan.cap, PACK) + c, 1)
        tallies[at, :] = jnp.full((1, lanes), count, jnp.int32)
        return 0

    lax.fori_loop(0, blocks, step, 0)
    sum_rows = plan.cap * SUB
    tally_rows = round_up(plan.cap, PACK)
    for o in range(plan.shards):
        pay[o, plan.sum_at : plan.sum_at + sum_rows, :] = sums[
            o * sum_rows : (o + 1) * sum_rows, :
        ].astype(jnp.int16)
        pay[o, plan.count_at : plan.pay_rows, :] = tallies[
            o * tally_rows : (o + 1) * tally_rows, :
        ].astype(jnp.int16)


def minute_stats(plan, samples, counts, series, omap, after):
    blocks, rows, lanes = samples.shape
    return pl.pallas_call(
        functools.partial(stats_kernel, plan),
        out_shape=jax.ShapeDtypeStruct((plan.shards, plan.pay_rows, lanes), jnp.int16),
        in_specs=[SMEM, SMEM, SMEM, HBM, VMEM],
        out_specs=VMEM,
        scratch_shapes=[
            pltpu.VMEM((blocks, rows, lanes), jnp.bfloat16),
            pltpu.VMEM((plan.shards * plan.cap * SUB, lanes), jnp.int32),
            pltpu.VMEM((plan.shards * round_up(plan.cap, PACK), lanes), jnp.int32),
            pltpu.SMEM((plan.shards,), jnp.int32),
            pltpu.SemaphoreType.DMA((blocks,)),
        ],
        compiler_params=pltpu.CompilerParams(vmem_limit_bytes=57 * MIB),
        name="minute_stats",
    )(counts, series, omap, samples, after)


def decode_live(tile):
    low = tile[:SUB].astype(jnp.float32)
    return low + tile[SUB:].astype(jnp.float32) * float(LIVE_BASE)


def exchange_kernel(plan, step, lanes, *refs):
    last = step == plan.bits
    arrays = min(step, 2) * 2 + max(step - 2, 0)
    parts, coded, refs = refs[:2], refs[2 : 2 + arrays], refs[2 + arrays :]
    if step:
        live, refs = refs[0][...], refs[1:]
    else:
        top = plan.groups * BINS
        live = parts[0][top : top + SUB, :] + parts[1][top : top + SUB, :]
    outs, powers = refs[:-1], refs[-1]
    me = lax.axis_index("replica")
    mine = (me >> 1) * plan.shards + lax.axis_index("shard")
    received = []
    for a, ref in enumerate(coded):
        at, color = (a // 2, a % 2) if a < 4 else (a - 2, None)
        n = plan.count(at)
        tail = round_up(n, PACK)
        if not color:
            live = live + decode_live(ref[n * BINS + tail : n * BINS + tail + PACK, :])
        wide = ref[n * BINS : n * BINS + tail, :].astype(jnp.float32)
        powers[a + 2, :tail, :] = jnp.exp2(wide * (1.0 / 64)) * (1.0 / STEPS16)
        received.append((at, color, ref))
    ways = 1 if last else plan.ways(step)
    if step == 0:
        outs[2][...] = live
    for color in range(2):
        fixed = plan.settled(mine, color, min(step + 1, plan.bits), not last)
        for g in range(ways):
            j = fixed if last else fixed | plan.spread(g, color, step + 1)
            first = color * plan.ways(0) + plan.squeeze(j, color, 1)
            rows = pl.ds(pl.multiple_of(first * BINS, BINS), BINS)
            value = parts[0][rows, :] + parts[1][rows, :]
            for a, (at, its, ref) in enumerate(received):
                if its is None or its == color:
                    source = plan.squeeze(j, color, at + 1)
                    source = source if its == color else source * 2 + color
                    rows = pl.ds(pl.multiple_of(source * BINS, BINS), BINS)
                    power = powers[a + 2, pl.ds(source, 1), :]
                    value = value + ref[rows, :].astype(jnp.float32) * power
            if last:
                outs[0][color] = value
                continue
            which, to = (color, g) if step < 2 else (0, g * 2 + color)
            peak = jnp.max(jnp.abs(value), axis=0, keepdims=True)
            power = jnp.floor(jnp.log2(jnp.maximum(peak, 2.0**-126)) * 64.0) + 2.0
            powers[which, pl.ds(to, 1), :] = power
            value = value * jnp.exp2(power * (-1.0 / 64)) * STEPS16
            outs[which][to * BINS : (to + 1) * BINS, :] = to_int16(value)
    if last:
        sub = lax.broadcasted_iota(jnp.int32, (SUB, lanes), 0)
        place = sub * lanes + lax.broadcasted_iota(jnp.int32, (SUB, lanes), 1)
        for d in range(2):
            p = plan.position(mine, 0, me, d)
            outs[1][d] = jnp.sum(jnp.where(place == p, live, 0.0))
        return
    whole = live.astype(jnp.int32)
    high = whole // LIVE_BASE
    pair = jnp.concatenate([whole - high * LIVE_BASE, high], axis=0).astype(jnp.int16)
    n = plan.count(step)
    tail = round_up(n, PACK)
    for which in range(2 if step < 2 else 1):
        out = outs[which]
        out[n * BINS : n * BINS + tail, :] = (
            powers[which, :tail, :].astype(jnp.int32).astype(jnp.int16)
        )
        out[n * BINS + tail : n * BINS + tail + PACK, :] = pair


def exchange(plan, step, arrays):
    lanes = arrays[0].shape[-1]
    coded = min(step, 2) * 2 + max(step - 2, 0)
    if step == plan.bits:
        out_shape = (
            jax.ShapeDtypeStruct((2, BINS, lanes), jnp.float32),
            jax.ShapeDtypeStruct((2,), jnp.float32),
        )
        out_specs = (VMEM, SMEM)
    else:
        out_shape = [jax.ShapeDtypeStruct((plan.rows(step), lanes), jnp.int16)]
        if step < 2:
            out_shape = out_shape * 2
        if step == 0:
            out_shape = out_shape + [jax.ShapeDtypeStruct((SUB, lanes), jnp.float32)]
        out_specs = [VMEM] * len(out_shape)
    tail = max(round_up(plan.count(a), PACK) for a in range(plan.bits))
    return pl.pallas_call(
        functools.partial(exchange_kernel, plan, step, lanes),
        out_shape=tuple(out_shape),
        in_specs=[VMEM] * len(arrays),
        out_specs=tuple(out_specs),
        scratch_shapes=[pltpu.VMEM((2 + coded, tail, lanes), jnp.float32)],
        compiler_params=pltpu.CompilerParams(vmem_limit_bytes=16 * MIB),
    )(*arrays)


def cold_kernel(plan, pay, out, stage, sem):
    lanes = out.shape[-1]
    sub = lax.broadcasted_iota(jnp.int32, (SUB, lanes), 0)
    unit = LIMIT / STEPS16

    def copies(o):
        at = pl.ds(o * plan.cap, plan.cap)
        return pltpu.make_async_copy(stage.at[o % 2], out.at[at], sem.at[o % 2])

    for o in range(plan.shards):
        if o >= 2:
            copies(o - 2).wait()
        tally = pay[o, plan.count_at : plan.pay_rows, :].astype(jnp.int32)
        for c in range(plan.cap):
            if c % 2 == 0:
                at = plan.sum_at + c * SUB
                means = pay[o, at : at + PACK, :].astype(jnp.float32) * unit
            count = jnp.broadcast_to(tally[c : c + 1, :], (SUB, lanes))
            n = jnp.clip(count - MINUTE * sub, 0, MINUTE).astype(jnp.float32)
            filled = n > 0
            ends = pay[o, c * 2 * SUB : (c + 1) * 2 * SUB, :].astype(jnp.float32) * unit
            stage[o % 2, c, 0] = jnp.where(filled, ends[:SUB], 0.0)
            stage[o % 2, c, 1] = jnp.where(filled, ends[SUB:], 0.0)
            stage[o % 2, c, 2] = means[(c % 2) * SUB : (c % 2 + 1) * SUB] * n
            stage[o % 2, c, 3] = n
        copies(o).start()
    for o in range(max(0, plan.shards - 2), plan.shards):
        copies(o).wait()


def cold(plan, pay, minutes):
    shards, _, lanes = pay.shape
    return pl.pallas_call(
        functools.partial(cold_kernel, plan),
        out_shape=jax.ShapeDtypeStruct((shards * plan.cap, 4, minutes, lanes), jnp.float32),
        in_specs=[VMEM],
        out_specs=ANY,
        scratch_shapes=[
            pltpu.VMEM((2, plan.cap, 4, minutes, lanes), jnp.float32),
            pltpu.SemaphoreType.DMA((2,)),
        ],
        compiler_params=pltpu.CompilerParams(vmem_limit_bytes=8 * MIB),
        name="cold",
    )(pay)


def body(samples, counts, buckets, series, omap):
    blocks, rows, _ = samples.shape
    plan = Plan(lax.axis_size("shard"), lax.axis_size("replica"), omap.shape[0], blocks)

    def swap(bit, x):
        return lax.ppermute(x, *plan.partner(bit))

    send, keep, send_near, keep_near = sketch(plan, samples, counts, buckets, series, omap)
    far = [keep, swap(-1, send)]
    near = [keep_near, swap(-1, send_near)]
    *sent, live = exchange(plan, 0, far)
    bits = [order[0] for order in plan.orders]
    coded = [swap(bits[color], sent[color]) for color in range(2)]
    pay = minute_stats(plan, samples, counts, series, omap, live)
    pay = lax.all_to_all(pay, "shard", split_axis=0, concat_axis=0, tiled=True)
    for step in range(1, plan.bits):
        sent = exchange(plan, step, [*near, *coded, live])
        bits = [order[step] for order in plan.orders]
        coded += [swap(bits[i], x) for i, x in enumerate(sent)]
    sketches, live_rows = exchange(plan, plan.bits, [*near, *coded, live])
    stats = cold(plan, pay, rows // MINUTE)
    return stats.reshape((1, 1) + stats.shape), sketches, live_rows


def solution(mesh):
    both = ("shard", "replica")
    return jax.shard_map(
        body,
        mesh=mesh,
        in_specs=(P(both, None, None), P(both), P(both, None), P(both), P()),
        out_specs=(
            P("shard", "replica", None, None, None, None),
            P(both, None, None),
            P(both),
        ),
        check_vma=False,
    )
```
